32 devices in a mesh: group: 2 (over x), tile: 16 (over z, y, core).
Axes of the slice: x: 2, y: 2, z: 4, core: 2. Of those that a mesh axis runs over, the one named last changes fastest.
Arguments:
- residual: bfloat16 [4096, 128], P(('group', 'tile')), parts along dimension 0, may hold values from -6 to 6
- chosen: int32 [512], P(('group', 'tile')), parts along dimension 0, may hold values 0 or 1
- footprint_tile: int32 [2048, 4], P('tile'), may hold values from 0 to 15, all different within a row; in each aligned block of 128 rows (0 to 127, 128 to 255, ...) at most 32 rows name the same one
- footprint_block: int32 [2048, 4], P('tile'), may hold values from 0 to 6143
- interp: float32 [128, 128], replicated, may hold values from -0.5 to 0.5
- speed: float32 [64, 384, 512], P('tile'), may hold values from 0.25 to 1
Outputs:
- adjoint_field: float32 [128, 384, 512], P(('group', 'tile')), parts along dimension 0
- partials: float32 [4096, 128], P(('group', 'tile')), parts along dimension 0
The draws below stay inside these ranges and needn't reach their ends.
There are 2 independent parts, one for each index of `group`. The reference program is written for one: setup_inputs(seed, part) draws one part's arguments, and reference() takes and returns one part's arrays. A program takes and returns all parts, laid end to end along the dimension named above; an argument that names none is the same for every part. Nothing has to cross between parts.
Inputs may be any that keep to these rules, and one draw needn't show every extreme that they name: `footprint_tile`: the 4 tiles of a row differ; within the rows of one device no tile is named by more than 32 rows, a bound that some block reaches.
All inputs are finite; a program needn't handle non-finite values. No bound on the sum of `chosen` on one device may be relied on, other than what follows from the above.
Results may differ from the reference program's by a relative error of at most 0.0014.
Values may be sent and summed in bfloat16 or wider, within the bound.
A program may use at most 128 MiB of HBM per device.

```python
import math
import jax
import jax.numpy as jnp
import numpy as np
from jax import lax

SAMP = 128
NBLK = 8
TOP = 4
CAP = 32
STEPS = 4
NY = 384
NZ = 512
SENSORS = 256
ROWS_DEV = 128
ROWS = 2048
NX = 64
CBLK = 6144
N_TILE = 16


def plant(drawn, stream_key, smallest, high):
    dims = drawn.shape
    index_at = [jax.random.randint(jax.random.fold_in(stream_key, axis), (), 0, dims[axis]) for axis in range(len(dims))]
    drawn = drawn.at[tuple(index_at)].set(smallest)
    longest = dims.index(max(dims))
    index_at[longest] = (index_at[longest] + 1) % dims[longest]
    return drawn.at[tuple(index_at)].set(high)


def block_scale(rng, extent, cuts, smallest, top_value):
    factor_of, own = 1.0, jax.random.fold_in(rng, 6)
    for dim, parts in cuts:
        heights = jnp.exp(jax.random.uniform(jax.random.fold_in(own, dim), (parts,), jnp.float32, smallest / len(cuts), top_value / len(cuts)))
        factor_of = factor_of * jnp.repeat(heights, extent[dim] // parts).reshape([-1 if axis == dim else 1 for axis in range(len(extent))])
    return factor_of


def routed_block(rng, own, number, rows, number_of, top, most, skew):
    sequence = jax.random.permutation(rng, number_of)
    heavy_load, common = shares(number_of, rows * top, most, skew, True), shares(number_of, rows * top, most, skew, False)
    places = jnp.arange(number_of)

    def named(lengths, rotation):
        used = int((lengths > 0).sum())
        fixed = max(1, used // 4)
        shifted = fixed + (places - fixed + rotation * (used - fixed)) % max(1, number_of - fixed)
        return jnp.zeros((number_of,), jnp.int32).at[sequence[jnp.where(places < fixed, places, shifted)]].set(jnp.asarray(lengths, jnp.int32))

    lengths = jnp.where(number % 4 == 0, named(heavy_load, number // 4), named(common, number - number // 4 - 1))
    mixed = jax.random.permutation(jax.random.fold_in(own, 3), number_of)
    source_of, sink = mixed[0:number_of // 2 * 2:2], mixed[1:number_of // 2 * 2:2]
    slack = jnp.minimum(lengths[source_of] - 1, most - lengths[sink]) // 2
    slack = jnp.where((source_of == sequence[0]) | (sink == sequence[0]) | (lengths[sink] == 0), 0, jnp.maximum(slack, 0))
    shifted = jax.random.randint(jax.random.fold_in(own, 4), (number_of // 2,), 0, 1 << 20) % (slack + 1)
    lengths = lengths.at[source_of].add(-shifted).at[sink].add(shifted)
    items = jnp.searchsorted(jnp.cumsum(lengths), jnp.arange(rows * top), side="right").astype(jnp.int32)
    listing = items.reshape(top, rows).T
    listing = listing[jax.random.permutation(jax.random.fold_in(own, 1), rows)]
    rotation = jax.random.randint(jax.random.fold_in(own, 2), (rows, 1), 0, top)
    return jnp.take_along_axis(listing, (jnp.arange(top)[None, :] + rotation) % top, axis=1)


def shares(number_of, total, most, lean, full):
    portions = [(1 << 20) // math.isqrt(standing ** lean) + 1 for standing in range(1, number_of + 1)]
    largest = most if full else min(most, max(-(-total // number_of), total * portions[0] // sum(portions)))
    least = 1 if total - largest >= number_of - 1 else 0
    given, surplus = [largest] + [least] * (number_of - 1), total - largest - least * (number_of - 1)
    while surplus > 0:
        movable = [i for i in range(1, number_of) if given[i] < largest] or [i for i in range(1, number_of) if given[i] < most]
        mass, remaining = sum([portions[i] for i in movable]), surplus
        for i in movable:
            addition = min(most - given[i], max(1, remaining * portions[i] // mass), surplus)
            given[i] = given[i] + addition
            surplus = surplus - addition
    return np.array(given)


def scatter_about(rng, dims, scale, bound, pieces=(), dtype=jnp.bfloat16):
    loudness = block_scale(rng, dims, pieces, -0.22, 0.18) if pieces else 1.0
    drawn = jax.random.normal(rng, dims, jnp.float32) * scale * loudness
    return jnp.minimum(jnp.maximum(drawn, -bound), bound).astype(dtype)


def setup_inputs(seed: int = 0, part: int = 0) -> dict:
    streams_of = jax.random.split(jax.random.key(seed), 7)
    own_keys = jax.random.split(jax.random.fold_in(streams_of[6], part), 7)
    residual = scatter_about(own_keys[0], (ROWS, SAMP), 1.0, 6.0, ((0, 16),))
    chosen = plant((jax.random.randint(own_keys[1], (SENSORS,), 0, 2) < 1).astype(jnp.int32), jax.random.fold_in(own_keys[1], 1), 0, 1)
    footprint_tile_keys = jax.random.split(jax.random.fold_in(streams_of[2], 1), ROWS // ROWS_DEV)
    footprint_tile_turns = jax.random.permutation(jax.random.fold_in(streams_of[2], 3), ROWS // ROWS_DEV)
    footprint_tile = jax.vmap(lambda own, number: routed_block(jax.random.fold_in(streams_of[2], 2), own, number, ROWS_DEV, N_TILE, TOP, CAP, 2))(footprint_tile_keys, footprint_tile_turns).reshape((ROWS, TOP))
    footprint_block = plant(jax.random.randint(streams_of[3], (ROWS, TOP), 0, CBLK), jax.random.fold_in(streams_of[3], 1), 0, CBLK - 1).astype(jnp.int32)
    interp = scatter_about(streams_of[4], (SAMP, SAMP), SAMP ** -0.5, 0.5, (), jnp.float32)
    speed = jnp.clip(jnp.exp(math.log(1.0) - 1.3862944 * jax.random.uniform(streams_of[5], (NX, NY, NZ), jnp.float32) ** block_scale(streams_of[5], (NX, NY, NZ), ((0, 16),), -0.2, 0.2)), 0.25, 1.0)
    return dict(residual=residual, chosen=chosen, footprint_tile=footprint_tile, footprint_block=footprint_block, interp=interp, speed=speed)


pseudo_rate = 0.16


def smooth_step(field, speed):
    padded = jnp.pad(field, 1)
    beside = padded[2:, 1:-1, 1:-1] + padded[:-2, 1:-1, 1:-1]
    beside = beside + padded[1:-1, 2:, 1:-1] + padded[1:-1, :-2, 1:-1]
    beside = beside + padded[1:-1, 1:-1, 2:] + padded[1:-1, 1:-1, :-2]
    return field + pseudo_rate * speed * (beside - 6.0 * field)


def reference(residual, chosen, footprint_tile, footprint_block, interp, speed):
    rows = residual.shape[0]
    keep = jnp.repeat(chosen, NBLK).astype(jnp.bfloat16)
    traces = residual * keep[:, None]
    injected = jnp.dot(traces.astype(jnp.float32), interp, precision=lax.Precision.HIGHEST)
    target = (footprint_tile * CBLK + footprint_block).reshape(-1).astype(jnp.int32)
    values = jnp.broadcast_to(injected[:, None, :], (rows, TOP, SAMP)).reshape(-1, SAMP)
    source = jax.ops.segment_sum(values, target, num_segments=N_TILE * CBLK)
    field = source.reshape(NX, NY, NZ)
    for step in range(STEPS):
        field = smooth_step(field, speed)
    blocks = field.reshape(-1, SAMP)
    sampled = jnp.dot(blocks[target], interp.T, precision=lax.Precision.HIGHEST)
    partials = jnp.sum(sampled.reshape(rows, TOP, SAMP), axis=1)
    return field, partials
```

```python
import functools

import jax
import jax.numpy as jnp
from jax import lax
from jax.experimental import pallas as pl
from jax.experimental.pallas import tpu as pltpu
from jax.sharding import PartitionSpec as P

CAP = 32
STEPS = 4
RATE = 0.16
HALO = STEPS - 1
MESH = pl.DeviceIdType.MESH
VMEM = pl.BlockSpec(memory_space=pltpu.VMEM)
SMEM = pl.BlockSpec(memory_space=pltpu.SMEM)
F32 = jnp.float32
BF16 = jnp.bfloat16
HIGH = lax.Precision.HIGHEST


def iota(shape, dim):
    return lax.broadcasted_iota(jnp.int32, shape, dim)


def last_dims(a, b):
    return lax.dot_general(a, b, (((1,), (1,)), ((), ())), preferred_element_type=F32)


def dot32(a, b):
    return lax.dot_general(a, b, (((1,), (0,)), ((), ())), preferred_element_type=F32)


def slot_rows(dest, tiles):
    top, rows = dest.shape
    upper = (iota((rows, rows), 0) < iota((rows, rows), 1)).astype(BF16)
    base = jnp.zeros((tiles, 1), F32)
    out = []
    for k in range(top):
        here = dest[k : k + 1, :]
        hot = (iota((tiles, rows), 0) == here).astype(F32)
        ahead = dot32(hot.astype(BF16), upper) + base
        rank = jnp.sum(hot * ahead, axis=0, keepdims=True).astype(jnp.int32)
        base = base + jnp.sum(hot, axis=1, keepdims=True)
        out.append((hot, rank, here * CAP + rank))
    return out


def pack_kernel(tiles, geom, res_ref, chosen_ref, ft_ref, fb_ref, speed_ref, pay_ref, cod_ref, sp_ref):
    cx, ny, nz = geom
    nzb = nz // 128
    per_layer = ny * nzb
    top, rows = ft_ref.shape
    sensors = chosen_ref.shape[0]
    lane = iota((1, rows), 1)
    keep = jnp.zeros((1, rows), jnp.int32)
    for i in range(sensors):
        keep = jnp.where(lane // (rows // sensors) == i, chosen_ref[i], keep)
    keep = keep.astype(F32)
    block = fb_ref[...]
    layer = jnp.zeros_like(block)
    for i in range(1, cx):
        layer = layer + (block >= i * per_layer).astype(jnp.int32)
    in_layer = block - layer * per_layer
    y = in_layer // nzb
    zb = in_layer - y * nzb
    strip = layer * (ny // 8 + 1) + 1 + y // 8
    flat = (strip * nzb + zb) * 8 + (y - y // 8 * 8)
    hi = (flat // 64).astype(F32)
    lo = (flat - flat // 64 * 64).astype(F32)
    slots = slot_rows(ft_ref[...], tiles)
    place = jnp.zeros((tiles * CAP, rows), F32)
    codes = jnp.zeros((tiles, 128), F32)
    for k, (hot, rank, slot) in enumerate(slots):
        place = place + (iota((tiles * CAP, rows), 0) == slot).astype(F32)
        at = (iota((128, rows), 0) == rank).astype(BF16)
        upper = last_dims((hot * hi[k : k + 1]).astype(BF16), at)
        lower = last_dims((hot * lo[k : k + 1]).astype(BF16), at)
        codes = codes + upper * 64.0 + lower
    payload = dot32((place * keep).astype(BF16), res_ref[...]).astype(BF16)
    pay_ref[0] = jnp.zeros((CAP, 128), BF16)
    pay_ref[tiles + 1] = jnp.zeros((CAP, 128), BF16)
    pay_ref[1 : tiles + 1] = payload.reshape(tiles, CAP, 128)
    codes = codes.astype(jnp.int32)
    cod_ref[0] = jnp.zeros((1, 128), jnp.int32)
    cod_ref[tiles + 1] = jnp.zeros((1, 128), jnp.int32)
    for d in range(tiles):
        cod_ref[1 + d] = codes[d : d + 1]
    for l in range(cx):
        sp_ref[l] = speed_ref[l].astype(BF16)


def greet(n, me, partner=None):
    barrier = pltpu.get_barrier_semaphore()

    @pl.loop(1, n)
    def _(i):
        pl.semaphore_signal(barrier, inc=1, device_id={"tile": lax.rem(me + i, n)}, device_id_type=MESH)

    count = n - 1
    if partner is not None:
        pl.semaphore_signal(barrier, inc=1, device_id={"group": partner}, device_id_type=MESH)
        count += 1
    pl.semaphore_wait(barrier, count)


def send_kernel(n, groups, pay, cod, sp, got, gotc, halo, sems, csems, isem, fsem, dsem, lsem):
    me = lax.axis_index("tile")
    paired = groups % 2 == 0
    g = lax.axis_index("group")
    half = lax.rem(g, 2)
    partner = g + 1 - 2 * half if paired else None
    greet(n, me, partner)
    ny = sp.shape[1]
    rows = ny // 2 if paired else ny
    start = half * rows if paired else 0
    odd = lax.rem(me, 2)
    nb = me + 2 * odd - 1
    cb = me + 1 - 2 * odd
    inter = jnp.logical_and(nb >= 0, nb < n)
    window = pl.ds(start, rows)

    def piece(j):
        return pltpu.make_async_remote_copy(
            sp.at[odd + j, window], halo.at[1 - odd, j, window], isem.at[0, j], isem.at[1, j],
            device_id={"tile": nb}, device_id_type=MESH)

    def forward(j):
        return pltpu.make_async_remote_copy(
            halo.at[odd, j, window], halo.at[odd, j, window], fsem.at[0, j], fsem.at[1, j],
            device_id={"group": partner}, device_id_type=MESH)

    inside = pltpu.make_async_remote_copy(
        sp.at[pl.ds(1 - odd, HALO)], halo.at[odd], dsem.at[0], dsem.at[1],
        device_id={"tile": cb}, device_id_type=MESH)

    @pl.when(inter)
    def _():
        for j in range(HALO):
            piece(j).start()

    inside.start()

    def data(i):
        e = lax.rem(me + i, n)
        return pltpu.make_async_remote_copy(
            pay.at[pl.ds(e, 3)], got.at[me], sems.at[0, i], sems.at[1, i],
            device_id={"tile": e}, device_id_type=MESH)

    def code(i):
        e = lax.rem(me + i, n)
        return pltpu.make_async_remote_copy(
            cod.at[pl.ds(e, 3)], gotc.at[me], csems.at[0, i], csems.at[1, i],
            device_id={"tile": e}, device_id_type=MESH)

    @pl.loop(1, n)
    def _(i):
        data(i).start()
        code(i).start()

    own = pltpu.make_async_copy(pay.at[pl.ds(me, 3)], got.at[me], lsem.at[0])
    ownc = pltpu.make_async_copy(cod.at[pl.ds(me, 3)], gotc.at[me], lsem.at[1])
    own.start()
    ownc.start()

    @pl.when(jnp.logical_not(inter))
    def _():
        halo[odd] = jnp.zeros(halo.shape[1:], halo.dtype)

    if paired:
        @pl.when(inter)
        def _():
            for j in range(HALO):
                piece(j).wait_recv()
                forward(j).start()
            for j in range(HALO):
                piece(j).wait_send()
                forward(j).wait()
    else:
        @pl.when(inter)
        def _():
            for j in range(HALO):
                piece(j).wait()

    inside.wait()

    @pl.loop(1, n)
    def _(i):
        data(i).wait()
        code(i).wait()

    own.wait()
    ownc.wait()


def field_kernel(geom, got, codes, interp, speed, halo, field, sampled, ua, ub, vals):
    cx, ny, nz = geom
    nzb = nz // 128
    tile = nzb * 8
    strips = ny // 8
    pitch = strips + 1
    n = got.shape[0]
    span = 3 * CAP
    layers = 3 * cx
    per_tile = cx * pitch * tile
    vals[...] = jnp.dot(got[...].reshape(n * span, 128).astype(F32), interp[...], precision=HIGH)

    zero = jnp.zeros((tile, 128), F32)

    @pl.loop(0, layers * pitch + 1, unroll=4)
    def _(s):
        ua[pl.ds(pl.multiple_of(s * tile, tile), tile)] = zero

    for l in range(layers + 1):
        ub[l * pitch * tile : l * pitch * tile + tile] = zero

    @pl.loop(0, n)
    def _(s):
        for o in range(3):
            for j in range(CAP):
                at = codes[s * 3 + o, j] + o * per_tile
                ua[pl.ds(at, 1)] = ua[pl.ds(at, 1)] + vals[pl.ds(s * span + o * CAP + j, 1)]

    sub = iota((8, 128), 0)
    lane = iota((8, 128), 1)
    first_sub, last_sub = sub == 0, sub == 7
    first_lane, last_lane = lane == 0, lane == 127

    def layer_step(src, dst, l, rate_of, final):
        @pl.loop(0, strips // 2)
        def _(p):
            rates = [rate_of(p, zb) for zb in range(nzb)]
            for h in range(2):
                base = pl.multiple_of((l * pitch + 1 + p * 2 + h) * tile, tile)
                centre = [src[pl.ds(base + zb * 8, 8)] for zb in range(nzb)]
                for zb in range(nzb):
                    c = centre[zb]
                    before = src[pl.ds(base - tile + zb * 8, 8)]
                    after = src[pl.ds(base + tile + zb * 8, 8)]
                    left = centre[zb - 1] if zb > 0 else 0.0
                    right = centre[zb + 1] if zb + 1 < nzb else 0.0
                    total = src[pl.ds(base - pitch * tile + zb * 8, 8)] + src[pl.ds(base + pitch * tile + zb * 8, 8)]
                    total = total + pltpu.roll(jnp.where(last_sub, before, c), 1, 0)
                    total = total + pltpu.roll(jnp.where(first_sub, after, c), 7, 0)
                    total = total + pltpu.roll(jnp.where(last_lane, left, c), 1, 1)
                    total = total + pltpu.roll(jnp.where(first_lane, right, c), 127, 1)
                    new = c + rates[zb][h * 8 : h * 8 + 8] * (total - 6.0 * c)
                    dst[pl.ds(base + zb * 8, 8)] = new
                    if final is not None:
                        field[final, pl.ds(pl.multiple_of(p * 16 + h * 8, 8), 8), zb * 128 : zb * 128 + 128] = new

    def rate_from(ref, index):
        def rate_of(p, zb):
            rows = pl.ds(pl.multiple_of(p * 16, 16), 16)
            return RATE * ref[(*index, rows, slice(zb * 128, zb * 128 + 128))].astype(F32)
        return rate_of

    src, dst = ua, ub
    for step in range(STEPS):
        reach = STEPS - 1 - step
        for l in range(cx - reach, 2 * cx + reach):
            if l < cx:
                rate_of = rate_from(halo, (0, l - (cx - HALO)))
            elif l >= 2 * cx:
                rate_of = rate_from(halo, (1, l - 2 * cx))
            else:
                rate_of = rate_from(speed, (l - cx,))
            layer_step(src, dst, l, rate_of, l - cx if step == STEPS - 1 else None)
        src, dst = dst, src

    @pl.loop(0, n)
    def _(s):
        for j in range(CAP):
            at = codes[s * 3 + 1, j] + per_tile
            sampled[s, pl.ds(j, 1)] = src[pl.ds(at, 1)]


def return_kernel(n, sampled, ft, interp, out, ret, sems, lsem):
    me = lax.axis_index("tile")
    greet(n, me)

    def block(i):
        e = lax.rem(me + i, n)
        return pltpu.make_async_remote_copy(
            sampled.at[e], ret.at[me], sems.at[0, i], sems.at[1, i],
            device_id={"tile": e}, device_id_type=MESH)

    @pl.loop(1, n)
    def _(i):
        block(i).start()

    own = pltpu.make_async_copy(sampled.at[me], ret.at[me], lsem)
    own.start()
    rows = ft.shape[1]
    place = jnp.zeros((n * CAP, rows), F32)
    for hot, rank, slot in slot_rows(ft[...], n):
        place = place + (iota((n * CAP, rows), 0) == slot).astype(F32)
    own.wait()

    @pl.loop(1, n)
    def _(i):
        block(i).wait()

    total = lax.dot_general(
        place, ret[...].reshape(n * CAP, 128), (((0,), (0,)), ((), ())),
        precision=HIGH, preferred_element_type=F32)
    out[...] = lax.dot_general(
        total, interp[...], (((1,), (1,)), ((), ())), precision=HIGH, preferred_element_type=F32)


def body(groups, residual, chosen, footprint_tile, footprint_block, interp, speed):
    n = lax.axis_size("tile")
    cx, ny, nz = geom = speed.shape
    rows, samp = residual.shape
    shape = jax.ShapeDtypeStruct
    ft, fb = footprint_tile.T, footprint_block.T
    pay, cod, sp = pl.pallas_call(
        functools.partial(pack_kernel, n, geom),
        out_shape=(
            shape((n + 2, CAP, samp), BF16),
            shape((n + 2, 1, 128), jnp.int32),
            shape(geom, BF16),
        ),
        in_specs=[VMEM, SMEM, VMEM, VMEM, VMEM],
        out_specs=(VMEM, VMEM, VMEM),
        name="pack",
    )(residual, chosen, ft, fb, speed)
    dma = pltpu.SemaphoreType.DMA
    got, gotc, halo = pl.pallas_call(
        functools.partial(send_kernel, n, groups),
        out_shape=(
            shape((n, 3, CAP, samp), BF16),
            shape((n, 3, 1, 128), jnp.int32),
            shape((2, HALO, ny, nz), BF16),
        ),
        in_specs=[VMEM] * 3,
        out_specs=(VMEM,) * 3,
        scratch_shapes=[
            dma((2, n)), dma((2, n)), dma((2, HALO)), dma((2, HALO)), dma((2,)), dma((2,)),
        ],
        compiler_params=pltpu.CompilerParams(collective_id=0, has_side_effects=True),
        name="exchange",
    )(pay, cod, sp)
    flat = (3 * cx * (ny // 8 + 1) + 1) * (nz // 16)
    field, sampled = pl.pallas_call(
        functools.partial(field_kernel, geom),
        out_shape=(shape(geom, F32), shape((n, CAP, samp), F32)),
        in_specs=[VMEM, SMEM, VMEM, VMEM, VMEM],
        out_specs=(VMEM, VMEM),
        scratch_shapes=[
            pltpu.VMEM((flat, 128), F32), pltpu.VMEM((flat, 128), F32),
            pltpu.VMEM((n * 3 * CAP, 128), F32),
        ],
        name="field",
    )(got, gotc.reshape(n * 3, 128), interp, speed, halo)
    partials = pl.pallas_call(
        functools.partial(return_kernel, n),
        out_shape=shape((rows, samp), F32),
        in_specs=[VMEM] * 3,
        out_specs=VMEM,
        scratch_shapes=[pltpu.VMEM((n, CAP, samp), F32), dma((2, n)), dma],
        compiler_params=pltpu.CompilerParams(collective_id=1, has_side_effects=True),
        name="give_back",
    )(sampled, ft, interp)
    return field, partials


def solution(mesh):
    placed = (
        P(("group", "tile"), None),
        P(("group", "tile")),
        P("tile", None),
        P("tile", None),
        P(),
        P("tile", None, None),
    )
    return jax.shard_map(
        functools.partial(body, mesh.shape["group"]),
        mesh=mesh,
        in_specs=placed,
        out_specs=(P(("group", "tile"), None, None), P(("group", "tile"), None)),
        check_vma=False,
    )
```

```python
import functools

import jax
import jax.numpy as jnp
from jax import lax
from jax.experimental import pallas as pl
from jax.experimental.pallas import tpu as pltpu
from jax.sharding import PartitionSpec as P

CAP = 32
STEPS = 4
RATE = 0.16
HALO = STEPS - 1
MESH = pl.DeviceIdType.MESH
VMEM = pl.BlockSpec(memory_space=pltpu.VMEM)
SMEM = pl.BlockSpec(memory_space=pltpu.SMEM)
F32 = jnp.float32
BF16 = jnp.bfloat16
HIGH = lax.Precision.HIGHEST


def iota(shape, dim):
    return lax.broadcasted_iota(jnp.int32, shape, dim)


def last_dims(a, b):
    return lax.dot_general(a, b, (((1,), (1,)), ((), ())), preferred_element_type=F32)


def dot32(a, b):
    return lax.dot_general(a, b, (((1,), (0,)), ((), ())), preferred_element_type=F32)


def plane_rows(geom):
    return 3 * geom[0] * (geom[1] + 8) + 8


def slot_rows(dest, tiles):
    top, rows = dest.shape
    upper = (iota((rows, rows), 0) < iota((rows, rows), 1)).astype(BF16)
    base = jnp.zeros((tiles, 1), F32)
    out = []
    for k in range(top):
        here = dest[k : k + 1, :]
        hot = (iota((tiles, rows), 0) == here).astype(F32)
        ahead = dot32(hot.astype(BF16), upper) + base
        rank = jnp.sum(hot * ahead, axis=0, keepdims=True).astype(jnp.int32)
        base = base + jnp.sum(hot, axis=1, keepdims=True)
        out.append((hot, rank, here * CAP + rank))
    return out


def pack_kernel(tiles, geom, res_ref, chosen_ref, ft_ref, fb_ref, speed_ref, pay_ref, cod_ref, sp_ref):
    cx, ny, nz = geom
    nzb = nz // 128
    per_layer = ny * nzb
    top, rows = ft_ref.shape
    sensors = chosen_ref.shape[0]
    lane = iota((1, rows), 1)
    keep = jnp.zeros((1, rows), jnp.int32)
    for i in range(sensors):
        keep = jnp.where(lane // (rows // sensors) == i, chosen_ref[i], keep)
    keep = keep.astype(F32)
    block = fb_ref[...]
    layer = jnp.zeros_like(block)
    for i in range(1, cx):
        layer = layer + (block >= i * per_layer).astype(jnp.int32)
    in_layer = block - layer * per_layer
    y = in_layer // nzb
    zb = in_layer - y * nzb
    flat = zb * plane_rows(geom) + layer * (ny + 8) + 8 + y
    hi = (flat // 64).astype(F32)
    lo = (flat - flat // 64 * 64).astype(F32)
    slots = slot_rows(ft_ref[...], tiles)
    place = jnp.zeros((tiles * CAP, rows), F32)
    codes = jnp.zeros((tiles, 128), F32)
    for k, (hot, rank, slot) in enumerate(slots):
        place = place + (iota((tiles * CAP, rows), 0) == slot).astype(F32)
        at = (iota((128, rows), 0) == rank).astype(BF16)
        upper = last_dims((hot * hi[k : k + 1]).astype(BF16), at)
        lower = last_dims((hot * lo[k : k + 1]).astype(BF16), at)
        codes = codes + upper * 64.0 + lower
    payload = dot32((place * keep).astype(BF16), res_ref[...]).astype(BF16)
    pay_ref[0] = jnp.zeros((CAP, 128), BF16)
    pay_ref[tiles + 1] = jnp.zeros((CAP, 128), BF16)
    pay_ref[1 : tiles + 1] = payload.reshape(tiles, CAP, 128)
    codes = codes.astype(jnp.int32)
    cod_ref[0] = jnp.zeros((1, 128), jnp.int32)
    cod_ref[tiles + 1] = jnp.zeros((1, 128), jnp.int32)
    for d in range(tiles):
        cod_ref[1 + d] = codes[d : d + 1]
    for l in range(cx):
        sp_ref[l] = speed_ref[l].astype(BF16)


def greet(n, me, partner=None):
    barrier = pltpu.get_barrier_semaphore()

    @pl.loop(1, n)
    def _(i):
        pl.semaphore_signal(barrier, inc=1, device_id={"tile": lax.rem(me + i, n)}, device_id_type=MESH)

    count = n - 1
    if partner is not None:
        pl.semaphore_signal(barrier, inc=1, device_id={"group": partner}, device_id_type=MESH)
        count += 1
    pl.semaphore_wait(barrier, count)


def send_kernel(n, groups, pay, cod, sp, got, gotc, halo, sems, csems, isem, fsem, dsem, lsem):
    me = lax.axis_index("tile")
    paired = groups % 2 == 0
    g = lax.axis_index("group")
    half = lax.rem(g, 2)
    partner = g + 1 - 2 * half if paired else None
    greet(n, me, partner)
    ny = sp.shape[1]
    rows = ny // 2 if paired else ny
    start = half * rows if paired else 0
    odd = lax.rem(me, 2)
    nb = me + 2 * odd - 1
    cb = me + 1 - 2 * odd
    inter = jnp.logical_and(nb >= 0, nb < n)
    window = pl.ds(start, rows)

    def piece(j):
        return pltpu.make_async_remote_copy(
            sp.at[odd + j, window], halo.at[1 - odd, j, window], isem.at[0, j], isem.at[1, j],
            device_id={"tile": nb}, device_id_type=MESH)

    def forward(j):
        return pltpu.make_async_remote_copy(
            halo.at[odd, j, window], halo.at[odd, j, window], fsem.at[0, j], fsem.at[1, j],
            device_id={"group": partner}, device_id_type=MESH)

    inside = pltpu.make_async_remote_copy(
        sp.at[pl.ds(1 - odd, HALO)], halo.at[odd], dsem.at[0], dsem.at[1],
        device_id={"tile": cb}, device_id_type=MESH)

    @pl.when(inter)
    def _():
        for j in range(HALO):
            piece(j).start()

    inside.start()

    def data(i):
        e = lax.rem(me + i, n)
        return pltpu.make_async_remote_copy(
            pay.at[pl.ds(e, 3)], got.at[me], sems.at[0, i], sems.at[1, i],
            device_id={"tile": e}, device_id_type=MESH)

    def code(i):
        e = lax.rem(me + i, n)
        return pltpu.make_async_remote_copy(
            cod.at[pl.ds(e, 3)], gotc.at[me], csems.at[0, i], csems.at[1, i],
            device_id={"tile": e}, device_id_type=MESH)

    @pl.loop(1, n)
    def _(i):
        data(i).start()
        code(i).start()

    own = pltpu.make_async_copy(pay.at[pl.ds(me, 3)], got.at[me], lsem.at[0])
    ownc = pltpu.make_async_copy(cod.at[pl.ds(me, 3)], gotc.at[me], lsem.at[1])
    own.start()
    ownc.start()

    @pl.when(jnp.logical_not(inter))
    def _():
        halo[odd] = jnp.zeros(halo.shape[1:], halo.dtype)

    if paired:
        @pl.when(inter)
        def _():
            for j in range(HALO):
                piece(j).wait_recv()
                forward(j).start()
            for j in range(HALO):
                piece(j).wait_send()
                forward(j).wait()
    else:
        @pl.when(inter)
        def _():
            for j in range(HALO):
                piece(j).wait()

    inside.wait()

    @pl.loop(1, n)
    def _(i):
        data(i).wait()
        code(i).wait()

    own.wait()
    ownc.wait()


def field_kernel(geom, got, codes, interp, speed, halo, field, sampled, ua, ub, vals):
    cx, ny, nz = geom
    nzb = nz // 128
    pitch = ny + 8
    plane = plane_rows(geom)
    n = got.shape[0]
    span = 3 * CAP
    layers = 3 * cx
    per_tile = cx * pitch
    vals[...] = jnp.dot(got[...].reshape(n * span, 128).astype(F32), interp[...], precision=HIGH)

    zero = jnp.zeros((8, 128), F32)

    @pl.loop(0, nzb * plane // 8 // 19)
    def _(s):
        for i in range(19):
            ua[pl.ds(pl.multiple_of(s * 152 + i * 8, 8), 8)] = zero

    for row in range(nzb * plane // 152 * 152, nzb * plane, 8):
        ua[row : row + 8] = zero

    for zb in range(nzb):
        for l in range(layers + 1):
            row = zb * plane + l * pitch
            ub[row : row + 8] = zero

    @pl.loop(0, n)
    def _(s):
        for o in range(3):
            for j in range(CAP):
                at = codes[s * 3 + o, j] + o * per_tile
                ua[pl.ds(at, 1)] = ua[pl.ds(at, 1)] + vals[pl.ds(s * span + o * CAP + j, 1)]

    lane = iota((8, 128), 1)
    first_lane, last_lane = lane == 0, lane == 127
    strips = next(k for k in (6, 4, 2) if ny % (8 * k) == 0)

    def layer_step(src, dst, l, rate_of, final):
        @pl.loop(0, ny // (8 * strips))
        def _(p):
            rates = [rate_of(pl.multiple_of(p * 8 * strips, 16), zb, 8 * strips) for zb in range(nzb)]
            for h in range(strips):
                row = pl.multiple_of(p * 8 * strips + h * 8, 8)
                base = pl.multiple_of(l * pitch + 8 + row, 8)
                centre = [src[pl.ds(base + zb * plane, 8)] for zb in range(nzb)]
                for zb in range(nzb):
                    c = centre[zb]
                    at = base + zb * plane
                    left = centre[zb - 1] if zb > 0 else 0.0
                    right = centre[zb + 1] if zb + 1 < nzb else 0.0
                    total = src[pl.ds(at - pitch, 8)] + src[pl.ds(at + pitch, 8)]
                    total = total + (src[pl.ds(at - 1, 8)] + src[pl.ds(at + 1, 8)])
                    total = total + pltpu.roll(jnp.where(last_lane, left, c), 1, 1)
                    total = total + pltpu.roll(jnp.where(first_lane, right, c), 127, 1)
                    new = c + rates[zb][h * 8 : h * 8 + 8] * (total - 6.0 * c)
                    dst[pl.ds(at, 8)] = new
                    if final is not None:
                        field[final, pl.ds(row, 8), zb * 128 : zb * 128 + 128] = new

    def rate_from(ref, index):
        def rate_of(row, zb, size):
            return RATE * ref[(*index, pl.ds(row, size), slice(zb * 128, zb * 128 + 128))].astype(F32)
        return rate_of

    src, dst = ua, ub
    for step in range(STEPS):
        reach = STEPS - 1 - step
        for l in range(cx - reach, 2 * cx + reach):
            if l < cx:
                rate_of = rate_from(halo, (0, l - (cx - HALO)))
            elif l >= 2 * cx:
                rate_of = rate_from(halo, (1, l - 2 * cx))
            else:
                rate_of = rate_from(speed, (l - cx,))
            layer_step(src, dst, l, rate_of, l - cx if step == STEPS - 1 else None)
        src, dst = dst, src

    @pl.loop(0, n)
    def _(s):
        for j in range(CAP):
            at = codes[s * 3 + 1, j] + per_tile
            sampled[s, pl.ds(j, 1)] = src[pl.ds(at, 1)]


def return_kernel(n, sampled, ft, interp, out, ret, sems, lsem):
    me = lax.axis_index("tile")
    greet(n, me)

    def block(i):
        e = lax.rem(me + i, n)
        return pltpu.make_async_remote_copy(
            sampled.at[e], ret.at[me], sems.at[0, i], sems.at[1, i],
            device_id={"tile": e}, device_id_type=MESH)

    @pl.loop(1, n)
    def _(i):
        block(i).start()

    own = pltpu.make_async_copy(sampled.at[me], ret.at[me], lsem)
    own.start()
    rows = ft.shape[1]
    place = jnp.zeros((n * CAP, rows), F32)
    for hot, rank, slot in slot_rows(ft[...], n):
        place = place + (iota((n * CAP, rows), 0) == slot).astype(F32)
    own.wait()

    @pl.loop(1, n)
    def _(i):
        block(i).wait()

    total = lax.dot_general(
        place, ret[...].reshape(n * CAP, 128), (((0,), (0,)), ((), ())),
        precision=HIGH, preferred_element_type=F32)
    out[...] = lax.dot_general(
        total, interp[...], (((1,), (1,)), ((), ())), precision=HIGH, preferred_element_type=F32)


def body(groups, residual, chosen, footprint_tile, footprint_block, interp, speed):
    n = lax.axis_size("tile")
    cx, ny, nz = geom = speed.shape
    rows, samp = residual.shape
    shape = jax.ShapeDtypeStruct
    ft, fb = footprint_tile.T, footprint_block.T
    pay, cod, sp = pl.pallas_call(
        functools.partial(pack_kernel, n, geom),
        out_shape=(
            shape((n + 2, CAP, samp), BF16),
            shape((n + 2, 1, 128), jnp.int32),
            shape(geom, BF16),
        ),
        in_specs=[VMEM, SMEM, VMEM, VMEM, VMEM],
        out_specs=(VMEM, VMEM, VMEM),
        name="pack",
    )(residual, chosen, ft, fb, speed)
    dma = pltpu.SemaphoreType.DMA
    got, gotc, halo = pl.pallas_call(
        functools.partial(send_kernel, n, groups),
        out_shape=(
            shape((n, 3, CAP, samp), BF16),
            shape((n, 3, 1, 128), jnp.int32),
            shape((2, HALO, ny, nz), BF16),
        ),
        in_specs=[VMEM] * 3,
        out_specs=(VMEM,) * 3,
        scratch_shapes=[
            dma((2, n)), dma((2, n)), dma((2, HALO)), dma((2, HALO)), dma((2,)), dma((2,)),
        ],
        compiler_params=pltpu.CompilerParams(collective_id=0, has_side_effects=True),
        name="exchange",
    )(pay, cod, sp)
    flat = plane_rows(geom) * (nz // 128)
    field, sampled = pl.pallas_call(
        functools.partial(field_kernel, geom),
        out_shape=(shape(geom, F32), shape((n, CAP, samp), F32)),
        in_specs=[VMEM, SMEM, VMEM, VMEM, VMEM],
        out_specs=(VMEM, VMEM),
        scratch_shapes=[
            pltpu.VMEM((flat, 128), F32), pltpu.VMEM((flat, 128), F32),
            pltpu.VMEM((n * 3 * CAP, 128), F32),
        ],
        name="field",
    )(got, gotc.reshape(n * 3, 128), interp, speed, halo)
    partials = pl.pallas_call(
        functools.partial(return_kernel, n),
        out_shape=shape((rows, samp), F32),
        in_specs=[VMEM] * 3,
        out_specs=VMEM,
        scratch_shapes=[pltpu.VMEM((n, CAP, samp), F32), dma((2, n)), dma],
        compiler_params=pltpu.CompilerParams(collective_id=1, has_side_effects=True),
        name="give_back",
    )(sampled, ft, interp)
    return field, partials


def solution(mesh):
    placed = (
        P(("group", "tile"), None),
        P(("group", "tile")),
        P("tile", None),
        P("tile", None),
        P(),
        P("tile", None, None),
    )
    return jax.shard_map(
        functools.partial(body, mesh.shape["group"]),
        mesh=mesh,
        in_specs=placed,
        out_specs=(P(("group", "tile"), None, None), P(("group", "tile"), None)),
        check_vma=False,
    )
```

```python
import functools

import jax
import jax.numpy as jnp
from jax import lax
from jax.experimental import pallas as pl
from jax.experimental.pallas import tpu as pltpu
from jax.sharding import PartitionSpec as P

CAP = 32
STEPS = 4
RATE = 0.16
HALO = STEPS - 1
MESH = pl.DeviceIdType.MESH
VMEM = pl.BlockSpec(memory_space=pltpu.VMEM)
ANY = pl.BlockSpec(memory_space=pl.ANY)
SMEM = pl.BlockSpec(memory_space=pltpu.SMEM)
F32 = jnp.float32
BF16 = jnp.bfloat16
HIGH = lax.Precision.HIGHEST


def iota(shape, dim):
    return lax.broadcasted_iota(jnp.int32, shape, dim)


def last_dims(a, b):
    return lax.dot_general(a, b, (((1,), (1,)), ((), ())), preferred_element_type=F32)


def dot32(a, b):
    return lax.dot_general(a, b, (((1,), (0,)), ((), ())), preferred_element_type=F32)


def plane_rows(geom):
    return 3 * geom[0] * (geom[1] + 8) + 8


def slot_rows(dest, tiles):
    top, rows = dest.shape
    upper = (iota((rows, rows), 0) < iota((rows, rows), 1)).astype(BF16)
    base = jnp.zeros((tiles, 1), F32)
    out = []
    for k in range(top):
        here = dest[k : k + 1, :]
        hot = (iota((tiles, rows), 0) == here).astype(F32)
        ahead = dot32(hot.astype(BF16), upper) + base
        rank = jnp.sum(hot * ahead, axis=0, keepdims=True).astype(jnp.int32)
        base = base + jnp.sum(hot, axis=1, keepdims=True)
        out.append((hot, rank, here * CAP + rank))
    return out


def pack_kernel(tiles, geom, res_ref, chosen_ref, ft_ref, fb_ref, speed_ref, pay_ref, cod_ref, sp_ref):
    cx, ny, nz = geom
    nzb = nz // 128
    per_layer = ny * nzb
    top, rows = ft_ref.shape
    sensors = chosen_ref.shape[0]
    lane = iota((1, rows), 1)
    keep = jnp.zeros((1, rows), jnp.int32)
    for i in range(sensors):
        keep = jnp.where(lane // (rows // sensors) == i, chosen_ref[i], keep)
    keep = keep.astype(F32)
    block = fb_ref[...]
    layer = jnp.zeros_like(block)
    for i in range(1, cx):
        layer = layer + (block >= i * per_layer).astype(jnp.int32)
    in_layer = block - layer * per_layer
    y = in_layer // nzb
    zb = in_layer - y * nzb
    flat = zb * plane_rows(geom) + layer * (ny + 8) + 8 + y
    hi = (flat // 64).astype(F32)
    lo = (flat - flat // 64 * 64).astype(F32)
    slots = slot_rows(ft_ref[...], tiles)
    place = jnp.zeros((tiles * CAP, rows), F32)
    codes = jnp.zeros((tiles, 128), F32)
    for k, (hot, rank, slot) in enumerate(slots):
        place = place + (iota((tiles * CAP, rows), 0) == slot).astype(F32)
        at = (iota((128, rows), 0) == rank).astype(BF16)
        upper = last_dims((hot * hi[k : k + 1]).astype(BF16), at)
        lower = last_dims((hot * lo[k : k + 1]).astype(BF16), at)
        codes = codes + upper * 64.0 + lower
    payload = dot32((place * keep).astype(BF16), res_ref[...]).astype(BF16)
    pay_ref[0] = jnp.zeros((CAP, 128), BF16)
    pay_ref[tiles + 1] = jnp.zeros((CAP, 128), BF16)
    pay_ref[1 : tiles + 1] = payload.reshape(tiles, CAP, 128)
    codes = codes.astype(jnp.int32)
    cod_ref[0] = jnp.zeros((1, 128), jnp.int32)
    cod_ref[tiles + 1] = jnp.zeros((1, 128), jnp.int32)
    for d in range(tiles):
        cod_ref[1 + d] = codes[d : d + 1]
    for l in range(cx):
        sp_ref[l] = speed_ref[l].astype(BF16)


def greet(n, me, partner=None):
    barrier = pltpu.get_barrier_semaphore()

    @pl.loop(1, n)
    def _(i):
        pl.semaphore_signal(barrier, inc=1, device_id={"tile": lax.rem(me + i, n)}, device_id_type=MESH)

    count = n - 1
    if partner is not None:
        pl.semaphore_signal(barrier, inc=1, device_id={"group": partner}, device_id_type=MESH)
        count += 1
    pl.semaphore_wait(barrier, count)


def send_kernel(n, groups, pay, cod, sp, got, gotc, halo, sems, csems, isem, fsem, dsem, lsem):
    me = lax.axis_index("tile")
    paired = groups % 2 == 0
    g = lax.axis_index("group")
    half = lax.rem(g, 2)
    partner = g + 1 - 2 * half if paired else None
    greet(n, me, partner)
    ny = sp.shape[1]
    rows = ny // 2 if paired else ny
    start = half * rows if paired else 0
    odd = lax.rem(me, 2)
    nb = me + 2 * odd - 1
    cb = me + 1 - 2 * odd
    inter = jnp.logical_and(nb >= 0, nb < n)
    cuts = isem.shape[1] // HALO

    def window(i):
        return pl.ds(start + i % cuts * (rows // cuts), rows // cuts)

    def piece(i):
        return pltpu.make_async_remote_copy(
            sp.at[odd + i // cuts, window(i)], halo.at[1 - odd, i // cuts, window(i)], isem.at[0, i], isem.at[1, i],
            device_id={"tile": nb}, device_id_type=MESH)

    def forward(i):
        here = halo.at[odd, i // cuts, window(i)]
        return pltpu.make_async_remote_copy(
            here, here, fsem.at[0, i], fsem.at[1, i],
            device_id={"group": partner}, device_id_type=MESH)

    inside = pltpu.make_async_remote_copy(
        sp.at[pl.ds(1 - odd, HALO)], halo.at[odd], dsem.at[0], dsem.at[1],
        device_id={"tile": cb}, device_id_type=MESH)

    @pl.when(inter)
    def _():
        for j in range(HALO * cuts):
            piece(j).start()

    inside.start()

    def data(i):
        e = lax.rem(me + i, n)
        return pltpu.make_async_remote_copy(
            pay.at[pl.ds(e, 3)], got.at[me], sems.at[0, i], sems.at[1, i],
            device_id={"tile": e}, device_id_type=MESH)

    def code(i):
        e = lax.rem(me + i, n)
        return pltpu.make_async_remote_copy(
            cod.at[pl.ds(e, 3)], gotc.at[me], csems.at[0, i], csems.at[1, i],
            device_id={"tile": e}, device_id_type=MESH)

    @pl.loop(1, n)
    def _(i):
        data(i).start()
        code(i).start()

    own = pltpu.make_async_copy(pay.at[pl.ds(me, 3)], got.at[me], lsem.at[0])
    ownc = pltpu.make_async_copy(cod.at[pl.ds(me, 3)], gotc.at[me], lsem.at[1])
    own.start()
    ownc.start()

    if paired:
        @pl.when(inter)
        def _():
            for j in range(HALO * cuts):
                piece(j).wait_recv()
                forward(j).start()
            for j in range(HALO * cuts):
                piece(j).wait_send()
                forward(j).wait()
    else:
        @pl.when(inter)
        def _():
            for j in range(HALO * cuts):
                piece(j).wait()

    inside.wait()

    @pl.loop(1, n)
    def _(i):
        data(i).wait()
        code(i).wait()

    own.wait()
    ownc.wait()


def field_kernel(
    geom, got, codes, interp, speed_in, halo_in, field, sampled, ua, ub, vals, speed, halo, made, in_sem, out_sem
):
    cx, ny, nz = geom
    nzb = nz // 128
    pitch = ny + 8
    plane = plane_rows(geom)
    n = got.shape[0]
    span = 3 * CAP
    layers = 3 * cx
    per_tile = cx * pitch
    me = lax.axis_index("tile")
    own = pltpu.make_async_copy(speed_in, speed, in_sem.at[2])
    own.start()
    for side, there in ((0, me > 0), (1, me < n - 1)):
        beside = pltpu.make_async_copy(halo_in.at[side], halo.at[side], in_sem.at[side])

        @pl.when(there)
        def _():
            beside.start()

        @pl.when(jnp.logical_not(there))
        def _():
            halo[side] = jnp.zeros(halo.shape[1:], halo.dtype)

    vals[...] = jnp.dot(got[...].reshape(n * span, 128).astype(F32), interp[...], precision=HIGH)

    zero = jnp.zeros((8, 128), F32)

    @pl.loop(0, nzb * plane // 8 // 19)
    def _(s):
        for i in range(19):
            ua[pl.ds(pl.multiple_of(s * 152 + i * 8, 8), 8)] = zero

    for row in range(nzb * plane // 152 * 152, nzb * plane, 8):
        ua[row : row + 8] = zero

    for zb in range(nzb):
        for l in range(layers + 1):
            row = zb * plane + l * pitch
            ub[row : row + 8] = zero

    @pl.loop(0, n)
    def _(s):
        for o in range(3):
            for j in range(CAP):
                at = codes[s * 3 + o, j] + o * per_tile
                ua[pl.ds(at, 1)] = ua[pl.ds(at, 1)] + vals[pl.ds(s * span + o * CAP + j, 1)]

    lane = iota((8, 128), 1)
    first_lane, last_lane = lane == 0, lane == 127
    def rate_at(l, row, zb):
        at = (0, l - (cx - HALO)) if l < cx else (1, l - 2 * cx)
        return RATE * halo[(*at, pl.ds(row, 16), slice(zb * 128, zb * 128 + 128))].astype(F32)

    def step_rows(src, dst, first, last, row, final):
        rates = {}
        for h in range(2):
            base = pl.multiple_of(row + 8 + h * 8, 8)

            def strip(l):
                return [src[pl.ds(base + l * pitch + zb * plane, 8)] for zb in range(nzb)]

            below, here = strip(first - 1), strip(first)
            for l in range(first, last):
                above = strip(l + 1)
                for zb in range(nzb):
                    if h == 0 and (l < cx or l >= 2 * cx):
                        rates[l, zb] = rate_at(l, row, zb)
                    c = here[zb]
                    at = base + l * pitch + zb * plane
                    left = here[zb - 1] if zb > 0 else 0.0
                    right = here[zb + 1] if zb + 1 < nzb else 0.0
                    total = below[zb] + above[zb]
                    total = total + (src[pl.ds(at - 1, 8)] + src[pl.ds(at + 1, 8)])
                    total = total + pltpu.roll(jnp.where(last_lane, left, c), 1, 1)
                    total = total + pltpu.roll(jnp.where(first_lane, right, c), 127, 1)
                    rate = rates[l, zb][h * 8 : h * 8 + 8] if l < cx or l >= 2 * cx else RATE * speed[l - cx, pl.ds(row + h * 8, 8), zb * 128 : zb * 128 + 128]
                    new = c + rate * (total - 6.0 * c)
                    dst[pl.ds(at, 8)] = new
                    if final:
                        made[l - cx, pl.ds(row + h * 8, 8), zb * 128 : zb * 128 + 128] = new
                below, here = here, above

    own.wait()
    for side, there in ((0, me > 0), (1, me < n - 1)):
        @pl.when(there)
        def _():
            pltpu.make_async_copy(halo_in.at[side], halo.at[side], in_sem.at[side]).wait()

    src, dst = ua, ub
    parts = out_sem.shape[0]
    size = ny // parts

    def give(part):
        rows = pl.ds(part * size, size)
        return pltpu.make_async_copy(made.at[:, rows], field.at[:, rows], out_sem.at[part])

    for step in range(STEPS):
        reach = STEPS - 1 - step
        final = step == STEPS - 1
        for part in range(parts if final else 1):
            start, stop = (part * size, part * size + size) if final else (0, ny)

            @pl.loop(start // 16, stop // 16)
            def _(p):
                step_rows(src, dst, cx - reach, 2 * cx + reach, pl.multiple_of(p * 16, 16), final)

            if final:
                give(part).start()
        src, dst = dst, src

    @pl.loop(0, n)
    def _(s):
        for j in range(CAP):
            at = codes[s * 3 + 1, j] + per_tile
            sampled[s, pl.ds(j, 1)] = src[pl.ds(at, 1)]

    for part in range(parts):
        give(part).wait()


def return_kernel(n, sampled, ft, interp, out, ret, sems, lsem):
    me = lax.axis_index("tile")
    greet(n, me)

    def block(i):
        e = lax.rem(me + i, n)
        return pltpu.make_async_remote_copy(
            sampled.at[e], ret.at[me], sems.at[0, i], sems.at[1, i],
            device_id={"tile": e}, device_id_type=MESH)

    @pl.loop(1, n)
    def _(i):
        block(i).start()

    own = pltpu.make_async_copy(sampled.at[me], ret.at[me], lsem)
    own.start()
    rows = ft.shape[1]
    place = jnp.zeros((n * CAP, rows), F32)
    for hot, rank, slot in slot_rows(ft[...], n):
        place = place + (iota((n * CAP, rows), 0) == slot).astype(F32)
    own.wait()

    @pl.loop(1, n)
    def _(i):
        block(i).wait()

    total = lax.dot_general(
        place, ret[...].reshape(n * CAP, 128), (((0,), (0,)), ((), ())),
        precision=HIGH, preferred_element_type=F32)
    out[...] = lax.dot_general(
        total, interp[...], (((1,), (1,)), ((), ())), precision=HIGH, preferred_element_type=F32)


def body(groups, residual, chosen, footprint_tile, footprint_block, interp, speed):
    n = lax.axis_size("tile")
    cx, ny, nz = geom = speed.shape
    rows, samp = residual.shape
    shape = jax.ShapeDtypeStruct
    ft, fb = footprint_tile.T, footprint_block.T
    pay, cod, sp = pl.pallas_call(
        functools.partial(pack_kernel, n, geom),
        out_shape=(
            shape((n + 2, CAP, samp), BF16),
            shape((n + 2, 1, 128), jnp.int32),
            shape(geom, BF16),
        ),
        in_specs=[VMEM, SMEM, VMEM, VMEM, VMEM],
        out_specs=(VMEM, VMEM, VMEM),
        name="pack",
    )(residual, chosen, ft, fb, speed)
    dma = pltpu.SemaphoreType.DMA
    got, gotc, halo = pl.pallas_call(
        functools.partial(send_kernel, n, groups),
        out_shape=(
            shape((n, 3, CAP, samp), BF16),
            shape((n, 3, 1, 128), jnp.int32),
            shape((2, HALO, ny, nz), BF16),
        ),
        in_specs=[VMEM, VMEM, ANY],
        out_specs=(VMEM, VMEM, ANY),
        scratch_shapes=[
            dma((2, n)), dma((2, n)), dma((2, 2 * HALO)), dma((2, 2 * HALO)), dma((2,)), dma((2,)),
        ],
        compiler_params=pltpu.CompilerParams(collective_id=0, has_side_effects=True),
        name="exchange",
    )(pay, cod, sp)
    flat = plane_rows(geom) * (nz // 128)
    field, sampled = pl.pallas_call(
        functools.partial(field_kernel, geom),
        out_shape=(shape(geom, F32), shape((n, CAP, samp), F32)),
        in_specs=[VMEM, SMEM, VMEM, ANY, ANY],
        out_specs=(ANY, VMEM),
        scratch_shapes=[
            pltpu.VMEM((flat, 128), F32), pltpu.VMEM((flat, 128), F32),
            pltpu.VMEM((n * 3 * CAP, 128), F32), pltpu.VMEM(geom, F32),
            pltpu.VMEM((2, HALO, ny, nz), BF16), pltpu.VMEM(geom, F32), dma((3,)), dma((3,)),
        ],
        name="field",
    )(got, gotc.reshape(n * 3, 128), interp, speed, halo)
    partials = pl.pallas_call(
        functools.partial(return_kernel, n),
        out_shape=shape((rows, samp), F32),
        in_specs=[VMEM] * 3,
        out_specs=VMEM,
        scratch_shapes=[pltpu.VMEM((n, CAP, samp), F32), dma((2, n)), dma],
        compiler_params=pltpu.CompilerParams(collective_id=1, has_side_effects=True),
        name="give_back",
    )(sampled, ft, interp)
    return field, partials


def solution(mesh):
    placed = (
        P(("group", "tile"), None),
        P(("group", "tile")),
        P("tile", None),
        P("tile", None),
        P(),
        P("tile", None, None),
    )
    return jax.shard_map(
        functools.partial(body, mesh.shape["group"]),
        mesh=mesh,
        in_specs=placed,
        out_specs=(P(("group", "tile"), None, None), P(("group", "tile"), None)),
        check_vma=False,
    )
```

```python
import functools

import jax
import jax.numpy as jnp
from jax import lax
from jax.experimental import pallas as pl
from jax.experimental.pallas import tpu as pltpu
from jax.sharding import PartitionSpec as P

CAP = 32
STEPS = 4
RATE = 0.16
HALO = STEPS - 1
MESH = pl.DeviceIdType.MESH
VMEM = pl.BlockSpec(memory_space=pltpu.VMEM)
ANY = pl.BlockSpec(memory_space=pl.ANY)
SMEM = pl.BlockSpec(memory_space=pltpu.SMEM)
F32 = jnp.float32
BF16 = jnp.bfloat16
HIGH = lax.Precision.HIGHEST


def iota(shape, dim):
    return lax.broadcasted_iota(jnp.int32, shape, dim)


def last_dims(a, b):
    return lax.dot_general(a, b, (((1,), (1,)), ((), ())), preferred_element_type=F32)


def dot32(a, b):
    return lax.dot_general(a, b, (((1,), (0,)), ((), ())), preferred_element_type=F32)


def plane_rows(geom):
    return 3 * geom[0] * (geom[1] + 8) + 8


def slot_rows(dest, tiles):
    top, rows = dest.shape
    upper = (iota((rows, rows), 0) < iota((rows, rows), 1)).astype(BF16)
    base = jnp.zeros((tiles, 1), F32)
    out = []
    for k in range(top):
        here = dest[k : k + 1, :]
        hot = (iota((tiles, rows), 0) == here).astype(F32)
        ahead = dot32(hot.astype(BF16), upper) + base
        rank = jnp.sum(hot * ahead, axis=0, keepdims=True).astype(jnp.int32)
        base = base + jnp.sum(hot, axis=1, keepdims=True)
        out.append((hot, rank, here * CAP + rank))
    return out


def pack_kernel(tiles, geom, res_ref, chosen_ref, ft_ref, fb_ref, speed_in, pay_ref, cod_ref, sp_out,
                speed_ref, sp_ref, in_sem, out_sem):
    cx, ny, nz = geom

    def take(l):
        return pltpu.make_async_copy(speed_in.at[l], speed_ref.at[l], in_sem.at[l])

    def give(l):
        return pltpu.make_async_copy(sp_ref.at[l], sp_out.at[l], out_sem.at[l])

    for l in range(cx):
        take(l).start()
    nzb = nz // 128
    per_layer = ny * nzb
    top, rows = ft_ref.shape
    sensors = chosen_ref.shape[0]
    lane = iota((1, rows), 1)
    keep = jnp.zeros((1, rows), jnp.int32)
    for i in range(sensors):
        keep = jnp.where(lane // (rows // sensors) == i, chosen_ref[i], keep)
    keep = keep.astype(F32)
    block = fb_ref[...]
    layer = jnp.zeros_like(block)
    for i in range(1, cx):
        layer = layer + (block >= i * per_layer).astype(jnp.int32)
    in_layer = block - layer * per_layer
    y = in_layer // nzb
    zb = in_layer - y * nzb
    flat = zb * plane_rows(geom) + layer * (ny + 8) + 8 + y
    hi = (flat // 64).astype(F32)
    lo = (flat - flat // 64 * 64).astype(F32)
    slots = slot_rows(ft_ref[...], tiles)
    place = jnp.zeros((tiles * CAP, rows), F32)
    codes = jnp.zeros((tiles, 128), F32)
    for k, (hot, rank, slot) in enumerate(slots):
        place = place + (iota((tiles * CAP, rows), 0) == slot).astype(F32)
        at = (iota((128, rows), 0) == rank).astype(BF16)
        upper = last_dims((hot * hi[k : k + 1]).astype(BF16), at)
        lower = last_dims((hot * lo[k : k + 1]).astype(BF16), at)
        codes = codes + upper * 64.0 + lower
    payload = dot32((place * keep).astype(BF16), res_ref[...]).astype(BF16)
    pay_ref[0] = jnp.zeros((CAP, 128), BF16)
    pay_ref[tiles + 1] = jnp.zeros((CAP, 128), BF16)
    pay_ref[1 : tiles + 1] = payload.reshape(tiles, CAP, 128)
    codes = codes.astype(jnp.int32)
    cod_ref[0] = jnp.zeros((1, 128), jnp.int32)
    cod_ref[tiles + 1] = jnp.zeros((1, 128), jnp.int32)
    for d in range(tiles):
        cod_ref[1 + d] = codes[d : d + 1]
    for l in range(cx):
        take(l).wait()
        sp_ref[l] = speed_ref[l].astype(BF16)
        give(l).start()
    for l in range(cx):
        give(l).wait()


def greet(n, me, partner=None):
    barrier = pltpu.get_barrier_semaphore()

    @pl.loop(1, n)
    def _(i):
        pl.semaphore_signal(barrier, inc=1, device_id={"tile": lax.rem(me + i, n)}, device_id_type=MESH)

    count = n - 1
    if partner is not None:
        pl.semaphore_signal(barrier, inc=1, device_id={"group": partner}, device_id_type=MESH)
        count += 1
    pl.semaphore_wait(barrier, count)


def send_kernel(n, groups, pay, cod, sp, got, gotc, halo, sems, csems, isem, fsem, dsem, lsem):
    me = lax.axis_index("tile")
    paired = groups % 2 == 0
    g = lax.axis_index("group")
    half = lax.rem(g, 2)
    partner = g + 1 - 2 * half if paired else None
    greet(n, me, partner)
    ny = sp.shape[1]
    rows = ny // 2 if paired else ny
    start = half * rows if paired else 0
    odd = lax.rem(me, 2)
    nb = me + 2 * odd - 1
    cb = me + 1 - 2 * odd
    inter = jnp.logical_and(nb >= 0, nb < n)
    cuts = isem.shape[1] // HALO

    def window(i):
        return pl.ds(start + i % cuts * (rows // cuts), rows // cuts)

    def piece(i):
        return pltpu.make_async_remote_copy(
            sp.at[odd + i // cuts, window(i)], halo.at[1 - odd, i // cuts, window(i)], isem.at[0, i], isem.at[1, i],
            device_id={"tile": nb}, device_id_type=MESH)

    def forward(i):
        here = halo.at[odd, i // cuts, window(i)]
        return pltpu.make_async_remote_copy(
            here, here, fsem.at[0, i], fsem.at[1, i],
            device_id={"group": partner}, device_id_type=MESH)

    inside = pltpu.make_async_remote_copy(
        sp.at[pl.ds(1 - odd, HALO)], halo.at[odd], dsem.at[0], dsem.at[1],
        device_id={"tile": cb}, device_id_type=MESH)

    @pl.when(inter)
    def _():
        for j in range(HALO * cuts):
            piece(j).start()

    inside.start()

    def data(i):
        e = lax.rem(me + i, n)
        return pltpu.make_async_remote_copy(
            pay.at[pl.ds(e, 3)], got.at[me], sems.at[0, i], sems.at[1, i],
            device_id={"tile": e}, device_id_type=MESH)

    def code(i):
        e = lax.rem(me + i, n)
        return pltpu.make_async_remote_copy(
            cod.at[pl.ds(e, 3)], gotc.at[me], csems.at[0, i], csems.at[1, i],
            device_id={"tile": e}, device_id_type=MESH)

    @pl.loop(1, n)
    def _(i):
        data(i).start()
        code(i).start()

    own = pltpu.make_async_copy(pay.at[pl.ds(me, 3)], got.at[me], lsem.at[0])
    ownc = pltpu.make_async_copy(cod.at[pl.ds(me, 3)], gotc.at[me], lsem.at[1])
    own.start()
    ownc.start()

    if paired:
        @pl.when(inter)
        def _():
            for j in range(HALO * cuts):
                piece(j).wait_recv()
                forward(j).start()
            for j in range(HALO * cuts):
                piece(j).wait_send()
                forward(j).wait()
    else:
        @pl.when(inter)
        def _():
            for j in range(HALO * cuts):
                piece(j).wait()

    inside.wait()

    @pl.loop(1, n)
    def _(i):
        data(i).wait()
        code(i).wait()

    own.wait()
    ownc.wait()


def field_kernel(
    geom, got, codes, interp, speed_in, halo_in, field, sampled, ua, ub, vals, speed, halo, made, in_sem, out_sem
):
    cx, ny, nz = geom
    nzb = nz // 128
    pitch = ny + 8
    plane = plane_rows(geom)
    n = got.shape[0]
    span = 3 * CAP
    layers = 3 * cx
    per_tile = cx * pitch
    me = lax.axis_index("tile")
    own = pltpu.make_async_copy(speed_in, speed, in_sem.at[2])
    own.start()
    for side, there in ((0, me > 0), (1, me < n - 1)):
        beside = pltpu.make_async_copy(halo_in.at[side], halo.at[side], in_sem.at[side])

        @pl.when(there)
        def _():
            beside.start()

        @pl.when(jnp.logical_not(there))
        def _():
            halo[side] = jnp.zeros(halo.shape[1:], halo.dtype)

    vals[...] = jnp.dot(got[...].reshape(n * span, 128).astype(F32), interp[...], precision=HIGH)

    zero = jnp.zeros((8, 128), F32)

    @pl.loop(0, nzb * plane // 8 // 19)
    def _(s):
        for i in range(19):
            ua[pl.ds(pl.multiple_of(s * 152 + i * 8, 8), 8)] = zero

    for row in range(nzb * plane // 152 * 152, nzb * plane, 8):
        ua[row : row + 8] = zero

    for zb in range(nzb):
        for l in range(layers + 1):
            row = zb * plane + l * pitch
            ub[row : row + 8] = zero

    @pl.loop(0, n)
    def _(s):
        for o in range(3):
            for j in range(CAP):
                at = codes[s * 3 + o, j] + o * per_tile
                ua[pl.ds(at, 1)] = ua[pl.ds(at, 1)] + vals[pl.ds(s * span + o * CAP + j, 1)]

    lane = iota((8, 128), 1)
    first_lane, last_lane = lane == 0, lane == 127
    def rate_at(l, row, zb):
        at = (0, l - (cx - HALO)) if l < cx else (1, l - 2 * cx)
        return RATE * halo[(*at, pl.ds(row, 16), slice(zb * 128, zb * 128 + 128))].astype(F32)

    def step_rows(src, dst, first, last, row, final):
        rates = {}
        for h in range(2):
            base = pl.multiple_of(row + 8 + h * 8, 8)

            def strip(l):
                return [src[pl.ds(base + l * pitch + zb * plane, 8)] for zb in range(nzb)]

            below, here = strip(first - 1), strip(first)
            for l in range(first, last):
                above = strip(l + 1)
                for zb in range(nzb):
                    if h == 0 and (l < cx or l >= 2 * cx):
                        rates[l, zb] = rate_at(l, row, zb)
                    c = here[zb]
                    at = base + l * pitch + zb * plane
                    left = here[zb - 1] if zb > 0 else 0.0
                    right = here[zb + 1] if zb + 1 < nzb else 0.0
                    total = below[zb] + above[zb]
                    total = total + (src[pl.ds(at - 1, 8)] + src[pl.ds(at + 1, 8)])
                    total = total + pltpu.roll(jnp.where(last_lane, left, c), 1, 1)
                    total = total + pltpu.roll(jnp.where(first_lane, right, c), 127, 1)
                    rate = rates[l, zb][h * 8 : h * 8 + 8] if l < cx or l >= 2 * cx else RATE * speed[l - cx, pl.ds(row + h * 8, 8), zb * 128 : zb * 128 + 128]
                    new = c + rate * (total - 6.0 * c)
                    dst[pl.ds(at, 8)] = new
                    if final:
                        made[l - cx, pl.ds(row + h * 8, 8), zb * 128 : zb * 128 + 128] = new
                below, here = here, above

    own.wait()
    for side, there in ((0, me > 0), (1, me < n - 1)):
        @pl.when(there)
        def _():
            pltpu.make_async_copy(halo_in.at[side], halo.at[side], in_sem.at[side]).wait()

    src, dst = ua, ub
    parts = out_sem.shape[0]
    size = ny // parts

    def give(part):
        rows = pl.ds(part * size, size)
        return pltpu.make_async_copy(made.at[:, rows], field.at[:, rows], out_sem.at[part])

    for step in range(STEPS):
        reach = STEPS - 1 - step
        final = step == STEPS - 1
        for part in range(parts if final else 1):
            start, stop = (part * size, part * size + size) if final else (0, ny)

            @pl.loop(start // 16, stop // 16)
            def _(p):
                step_rows(src, dst, cx - reach, 2 * cx + reach, pl.multiple_of(p * 16, 16), final)

            if final:
                give(part).start()
        src, dst = dst, src

    @pl.loop(0, n)
    def _(s):
        for j in range(CAP):
            at = codes[s * 3 + 1, j] + per_tile
            sampled[s, pl.ds(j, 1)] = src[pl.ds(at, 1)]

    for part in range(parts):
        give(part).wait()


def return_kernel(n, sampled, ft, out, ret, sems, lsem):
    me = lax.axis_index("tile")
    greet(n, me)

    def block(i):
        e = lax.rem(me + i, n)
        return pltpu.make_async_remote_copy(
            sampled.at[e], ret.at[me], sems.at[0, i], sems.at[1, i],
            device_id={"tile": e}, device_id_type=MESH)

    @pl.loop(1, n)
    def _(i):
        block(i).start()

    own = pltpu.make_async_copy(sampled.at[me], ret.at[me], lsem)
    own.start()
    rows = ft.shape[1]
    place = jnp.zeros((n * CAP, rows), F32)
    for hot, rank, slot in slot_rows(ft[...], n):
        place = place + (iota((n * CAP, rows), 0) == slot).astype(F32)
    own.wait()

    @pl.loop(1, n)
    def _(i):
        block(i).wait()

    out[...] = lax.dot_general(
        place, ret[...].reshape(n * CAP, 128), (((0,), (0,)), ((), ())),
        precision=HIGH, preferred_element_type=F32)


def body(groups, residual, chosen, footprint_tile, footprint_block, interp, speed):
    n = lax.axis_size("tile")
    cx, ny, nz = geom = speed.shape
    rows, samp = residual.shape
    shape = jax.ShapeDtypeStruct
    dma = pltpu.SemaphoreType.DMA
    ft, fb = footprint_tile.T, footprint_block.T
    pay, cod, sp = pl.pallas_call(
        functools.partial(pack_kernel, n, geom),
        out_shape=(
            shape((n + 2, CAP, samp), BF16),
            shape((n + 2, 1, 128), jnp.int32),
            shape(geom, BF16),
        ),
        in_specs=[VMEM, SMEM, VMEM, VMEM, ANY],
        out_specs=(VMEM, VMEM, ANY),
        scratch_shapes=[pltpu.VMEM(geom, F32), pltpu.VMEM(geom, BF16), dma((cx,)), dma((cx,))],
        name="pack",
    )(residual, chosen, ft, fb, speed)
    got, gotc, halo = pl.pallas_call(
        functools.partial(send_kernel, n, groups),
        out_shape=(
            shape((n, 3, CAP, samp), BF16),
            shape((n, 3, 1, 128), jnp.int32),
            shape((2, HALO, ny, nz), BF16),
        ),
        in_specs=[VMEM, VMEM, ANY],
        out_specs=(VMEM, VMEM, ANY),
        scratch_shapes=[
            dma((2, n)), dma((2, n)), dma((2, 2 * HALO)), dma((2, 2 * HALO)), dma((2,)), dma((2,)),
        ],
        compiler_params=pltpu.CompilerParams(collective_id=0, has_side_effects=True),
        name="exchange",
    )(pay, cod, sp)
    flat = plane_rows(geom) * (nz // 128)
    field, sampled = pl.pallas_call(
        functools.partial(field_kernel, geom),
        out_shape=(shape(geom, F32), shape((n, CAP, samp), F32)),
        in_specs=[VMEM, SMEM, VMEM, ANY, ANY],
        out_specs=(ANY, VMEM),
        scratch_shapes=[
            pltpu.VMEM((flat, 128), F32), pltpu.VMEM((flat, 128), F32),
            pltpu.VMEM((n * 3 * CAP, 128), F32), pltpu.VMEM(geom, F32),
            pltpu.VMEM((2, HALO, ny, nz), BF16), pltpu.VMEM(geom, F32), dma((3,)), dma((3,)),
        ],
        name="field",
    )(got, gotc.reshape(n * 3, 128), interp, speed, halo)
    summed = pl.pallas_call(
        functools.partial(return_kernel, n),
        out_shape=shape((rows, samp), F32),
        in_specs=[VMEM] * 2,
        out_specs=VMEM,
        scratch_shapes=[pltpu.VMEM((n, CAP, samp), F32), dma((2, n)), dma],
        compiler_params=pltpu.CompilerParams(collective_id=1, has_side_effects=True),
        name="give_back",
    )(sampled, ft)
    return field, jnp.dot(summed, interp.T, precision=HIGH)


def solution(mesh):
    placed = (
        P(("group", "tile"), None),
        P(("group", "tile")),
        P("tile", None),
        P("tile", None),
        P(),
        P("tile", None, None),
    )
    return jax.shard_map(
        functools.partial(body, mesh.shape["group"]),
        mesh=mesh,
        in_specs=placed,
        out_specs=(P(("group", "tile"), None, None), P(("group", "tile"), None)),
        check_vma=False,
    )
```
